32 devices in a mesh: depth: 4 (over y, x), gx: 2 (over core), gy: 4 (over z).
Axes of the slice: x: 2, y: 2, z: 4, core: 2. Of those that a mesh axis runs over, the one named last changes fastest.
Arguments:
- density: float32 [16, 64, 1024], P('depth', 'gx', 'gy'), may hold values from 0.1 to 1
- table_index: int32 [16, 64, 1024], P('depth', 'gx', 'gy'), may hold values from 0 to 255
- opacity_table: float32 [256], replicated, may hold values from 0.02 to 0.3
- color_table: float32 [3, 256], replicated, may hold values from 0.5 to 3
- light_direction: float32 [4, 3], replicated, may hold values from -4 to 4
- shear_offsets: int32 [4, 16, 2], replicated, may hold values from -16 to 16, as said below
Outputs:
- image: float32 [4, 4, 64, 1024], P('depth', None, 'gx', 'gy')
The draws below stay inside these ranges and needn't reach their ends.
Inputs may be any that keep to these rules, and one draw needn't show every extreme that they name: `shear_offsets`: every offset lies within -16 to 16; both ends occur in every draw.
All inputs are finite; a program needn't handle non-finite values.
Results may differ from the reference program's by a relative error of at most 0.000051.
Values sent between devices are 32-bit elements; how exact they have to be, the bound alone decides.
A program may use at most 64 MiB of HBM per device.

```python
import math
import jax
import jax.numpy as jnp
from jax import lax

LUT = 256
VIEWS = 4
MAXS = 16
NZ = 16
NX = 64
NY = 1024


def draw_shear_offsets(key, part):
    offsets = jax.random.randint(key, (VIEWS, NZ, 2), -MAXS, MAXS + 1)
    offsets = offsets.at[0, 0, 0].set(MAXS)
    offsets = offsets.at[VIEWS - 1, NZ - 1, 1].set(-MAXS)
    return offsets.astype(jnp.int32)


def plant(array, rng, least, high):
    place = [jax.random.randint(jax.random.fold_in(rng, axis), (), 0, length) for axis, length in enumerate(array.shape)]
    widest = array.shape.index(max(array.shape))
    neighbour = place[:widest] + [(place[widest] + 1) % array.shape[widest]] + place[widest + 1:]
    return array.at[tuple(place)].set(least).at[tuple(neighbour)].set(high)


def level_of(own_key, dims, split, low, high):
    def one(dim, parts):
        draws = jax.random.uniform(jax.random.fold_in(jax.random.fold_in(own_key, 6), dim), (parts,), jnp.float32, low / len(split), high / len(split))
        return jnp.repeat(jnp.exp(draws), dims[dim] // parts).reshape((-1,) + (1,) * (len(dims) - dim - 1))

    level = one(*split[0])
    for cut in split[1:]:
        level = level * one(*cut)
    return level


def scatter_about(own_key, dims, width, most, held_as=jnp.bfloat16):
    entries = jax.random.normal(own_key, dims, jnp.float32) * width
    return jnp.minimum(jnp.maximum(entries, -most), most).astype(held_as)


def setup_inputs(seed: int = 0) -> dict:
    keys = jax.random.split(jax.random.key(seed), 7)
    return {
        "density": jnp.clip(0.1 + 0.9 * jax.random.uniform(keys[0], (NZ, NX, NY), jnp.float32) ** level_of(keys[0], (NZ, NX, NY), ((0, 4), (1, 2), (2, 4)), -0.2, 0.2), 0.1, 1.0),
        "table_index": plant(jax.random.randint(keys[1], (NZ, NX, NY), 0, LUT), jax.random.fold_in(keys[1], 1), 0, LUT - 1).astype(jnp.int32),
        "opacity_table": jnp.clip(jnp.exp(jax.random.uniform(keys[2], (LUT,), jnp.float32, math.log(0.02), math.log(0.3))), 0.02, 0.3),
        "color_table": jnp.clip(jax.random.uniform(keys[3], (3, LUT), jnp.float32, 0.5, 3.0), 0.5, 3.0),
        "light_direction": scatter_about(keys[4], (VIEWS, 3), 1.0, 4.0, jnp.float32),
        "shear_offsets": draw_shear_offsets(jax.random.fold_in(keys[6], 71), 0),
    }


ambient = 0.3
diffuse = 0.7

def reference(density, table_index, opacity_table, color_table, light_direction, shear_offsets):
    padded = jnp.pad(density, 1)
    accums = [jnp.zeros((4, NX, NY), jnp.float32) for view in range(VIEWS)]
    for depth_pos in range(NZ):
        center = padded[depth_pos + 1]
        slope_depth = 0.5 * (padded[depth_pos + 2, 1:-1, 1:-1] - padded[depth_pos, 1:-1, 1:-1])
        slope_row = 0.5 * (center[2:, 1:-1] - center[:-2, 1:-1])
        slope_col = 0.5 * (center[1:-1, 2:] - center[1:-1, :-2])
        inner = center[1:-1, 1:-1]
        index_slice = table_index[depth_pos]
        kappa = opacity_table[index_slice]
        colors = color_table[:, index_slice]
        alpha = 1.0 - jnp.exp(-kappa * inner)
        base = alpha[None] * colors
        lengths = jnp.sqrt(slope_depth * slope_depth + slope_row * slope_row + slope_col * slope_col + 1.0)
        for view in range(VIEWS):
            light = light_direction[view]
            lambert = jnp.abs(light[0] * slope_depth + light[1] * slope_row + light[2] * slope_col) / lengths
            fragment = jnp.concatenate([alpha[None], base * (ambient + diffuse * lambert)[None]], axis=0)
            framed = jnp.pad(fragment, ((0, 0), (MAXS, MAXS), (MAXS, MAXS)))
            start_row = (MAXS - shear_offsets[view, depth_pos, 0]).astype(jnp.int32)
            start_col = (MAXS - shear_offsets[view, depth_pos, 1]).astype(jnp.int32)
            shifted = lax.dynamic_slice(framed, (jnp.int32(0), start_row, start_col), (4, NX, NY))
            accums[view] = accums[view] + (1.0 - accums[view][0:1]) * shifted
    return jnp.stack(accums)
```

```python
import functools

import jax
import jax.numpy as jnp
from jax import lax
from jax.experimental import pallas as pl
from jax.experimental.pallas import tpu as pltpu
from jax.sharding import PartitionSpec as P

MAXS = 16
LANES = 128
SUB = 8
GROUP = 32

ambient = 0.3
diffuse = 0.7

STEPS = (-1, 0, 1)
DIRS = [(z, x, y) for z in STEPS for x in STEPS for y in STEPS if (z, x, y) != (0, 0, 0)]


def flipped(value, mask):
    bit = 1
    while bit <= mask:
        if mask & bit:
            value = value + bit - 2 * bit * ((value // bit) % 2)
        bit *= 2
    return value


def kernel(
    sizes, dens_in, index_in, opacity_in, color_in, light_in, shear_in, others,
    opacity, color, light, shear, in_sem, wide_d, wide_i, edges, got_edges, got_depth, shaded, parts,
    send_sem, recv_sem, send2, recv2, part_send, part_recv,
):
    nd, nx, ny = sizes
    slices, rows, cols = dens_in.shape
    tiles = cols // LANES
    wide = cols + LANES
    halo = -(-(MAXS + 1) // SUB) * SUB
    low, high = halo, halo + rows
    me = (lax.axis_index("depth"), lax.axis_index("gx"), lax.axis_index("gy"))
    d = me[0]

    def there(step):
        ok = None
        for pos, s, n in zip(me, step, sizes):
            if s:
                one = (pos + s < n) if s > 0 else (pos + s >= 0)
                ok = one if ok is None else jnp.logical_and(ok, one)
        return ok

    def dev(step):
        return tuple(pos + s for pos, s in zip(me, step))

    masks = list(range(nd - 1, 0, -1))
    barrier = pltpu.get_barrier_semaphore()
    count = jnp.int32(0)
    for step in DIRS:
        ok = there(step)

        @pl.when(ok)
        def _():
            pl.semaphore_signal(barrier, inc=1, device_id=dev(step), device_id_type=pl.DeviceIdType.MESH)

        count = count + jnp.where(ok, 1, 0)
    for mask in masks:
        gap = flipped(d, mask) - d
        far = jnp.logical_or(gap > 1, gap < -1)

        @pl.when(far)
        def _():
            pl.semaphore_signal(
                barrier, inc=1, device_id=(flipped(d, mask), me[1], me[2]),
                device_id_type=pl.DeviceIdType.MESH,
            )

        count = count + jnp.where(far, 1, 0)

    dens = wide_d.at[pl.ds(1, slices), pl.ds(low, rows), pl.ds(0, cols)]
    index = wide_i.at[:, pl.ds(low, rows), pl.ds(0, cols)]
    loads = [
        pltpu.make_async_copy(src, dst, in_sem.at[k])
        for k, (src, dst) in enumerate((
            (dens_in, dens), (index_in, index), (opacity_in, opacity), (color_in, color),
            (light_in, light), (shear_in, shear),
        ))
    ]
    for load in loads:
        load.start()
    loads[0].wait()
    loads[1].wait()
    lane = lax.broadcasted_iota(jnp.int32, (SUB, LANES), 1)
    group = lane // GROUP
    for side in range(2):
        tile = tiles - 1 if side == 0 else 0
        for number, (ref, buf) in enumerate(((wide_d, 0), (wide_i, 1))):
            for z in range(slices):
                packed = None
                for r in range(rows // SUB):
                    v = ref[z + 1 - buf, low + r * SUB:low + (r + 1) * SUB, tile * LANES:(tile + 1) * LANES]
                    shift = (GROUP * r + (GROUP if side == 0 else 0)) % LANES
                    v = pltpu.roll(v, shift, 1) if shift else v
                    packed = v if packed is None else jnp.where(group == r, v, packed)
                edges[buf][side, z] = packed

    def src_rows(x, reach):
        return pl.ds(high - reach, reach) if x > 0 else (pl.ds(low, reach) if x < 0 else pl.ds(low, rows))

    def dst_rows(x, reach):
        return pl.ds(low - reach, reach) if x > 0 else (pl.ds(high, reach) if x < 0 else pl.ds(low, rows))

    def copies(number, step, only_dst=False):
        z, x, y = step
        side = 0 if y > 0 else 1
        if z == 0 and y == 0:
            pairs = [
                (wide_d.at[pl.ds(1, slices), src_rows(x, halo), pl.ds(0, cols)],
                 wide_d.at[pl.ds(1, slices), dst_rows(x, halo), pl.ds(0, cols)]),
                (wide_i.at[:, src_rows(x, MAXS), pl.ds(0, cols)], wide_i.at[:, dst_rows(x, MAXS), pl.ds(0, cols)]),
            ]
        elif z == 0:
            pairs = [
                (edges[0].at[side], got_edges[0].at[x + 1, side]),
                (edges[1].at[side], got_edges[1].at[x + 1, side]),
            ]
        else:
            edge = slices - 1 if z > 0 else 0
            slot = 0 if z > 0 else 1
            if y == 0:
                pairs = [(
                    wide_d.at[edge + 1, src_rows(x, MAXS), pl.ds(0, cols)],
                    wide_d.at[0 if z > 0 else slices + 1, dst_rows(x, MAXS), pl.ds(0, cols)],
                )]
            else:
                pairs = [(edges[0].at[side, edge], got_depth.at[slot, x + 1, side])]
        if only_dst:
            return [dst for _src, dst in pairs]
        made = []
        for (src, dst), (ss, rs) in zip(pairs, ((send_sem, recv_sem), (send2, recv2))):
            made.append(pltpu.make_async_remote_copy(
                src_ref=src, dst_ref=dst, send_sem=ss.at[number], recv_sem=rs.at[number],
                device_id=dev(step), device_id_type=pl.DeviceIdType.MESH,
            ))
        return made

    pl.semaphore_wait(barrier, count)
    order = sorted(range(len(DIRS)), key=lambda k: -sum(abs(s) for s in DIRS[k]))
    for number in order:
        step = DIRS[number]

        @pl.when(there(step))
        def _():
            for copy in copies(number, step):
                copy.start()

    for number in order:
        step = DIRS[number]
        back = tuple(-s for s in step)

        @pl.when(jnp.logical_not(there(back)))
        def _():
            for dst in copies(number, step, only_dst=True):
                dst[...] = jnp.zeros(dst.shape, dst.dtype)

    for load in loads[2:]:
        load.wait()

    entries = opacity.shape[0] // LANES
    tables = []
    for name in range(4):
        halves = []
        for e in range(entries):
            if name == 0:
                row = opacity[e * LANES:(e + 1) * LANES].reshape(1, LANES)
            else:
                row = color[name - 1:name, e * LANES:(e + 1) * LANES]
            halves.append(jnp.broadcast_to(row, (SUB, LANES)))
        tables.append(halves)

    def look(name, low_bits, part):
        value = None
        for e in range(entries):
            g = jnp.take_along_axis(tables[name][e], low_bits, axis=1, mode="promise_in_bounds")
            value = g if value is None else jnp.where(part >= e, g, value)
        return value

    offset = halo - MAXS

    def look_up(z, t, j):
        at = offset + t * SUB
        r0 = t * SUB
        cut = slice(j * LANES, (j + 1) * LANES)
        i = wide_i[z, at:at + SUB, cut]
        low_bits = jnp.bitwise_and(i, LANES - 1)
        part = jnp.right_shift(i, 7)
        alpha = 1.0 - jnp.exp(-look(0, low_bits, part) * wide_d[z + 1, at:at + SUB, cut])
        shaded[0, z, j, r0:r0 + SUB, :] = alpha
        for ch in range(3):
            shaded[1 + ch, z, j, r0:r0 + SUB, :] = alpha * look(1 + ch, low_bits, part)

    def slopes(z):
        for t in range(wide_tiles):
            at = offset + t * SUB
            r0 = t * SUB
            c = wide_d[z + 1, at:at + SUB, :]
            sd = wide_d[z + 2, at:at + SUB, :] - wide_d[z, at:at + SUB, :]
            sx = wide_d[z + 1, at + 1:at + 1 + SUB, :] - wide_d[z + 1, at - 1:at - 1 + SUB, :]
            sy = pltpu.roll(c, wide - 1, 1) - pltpu.roll(c, 1, 1)
            inv = lax.rsqrt(0.25 * (sd * sd + sx * sx + sy * sy) + 1.0) * (0.5 * diffuse)
            for j in range(wide // LANES):
                for k, slope in enumerate((sd, sx, sy)):
                    shaded[4 + k, z, j, r0:r0 + SUB, :] = (slope * inv)[:, j * LANES:(j + 1) * LANES]

    wide_tiles = (rows + 2 * MAXS) // SUB
    own = [
        (t, j) for t in range(MAXS // SUB, (MAXS + rows) // SUB) for j in range(tiles)
    ]
    rest = [
        (t, j) for t in range(wide_tiles) for j in range(tiles + 1) if (t, j) not in own
    ]

    def over_slices(first, last, body):
        def step(z, carry):
            body(z)
            return carry

        lax.fori_loop(first, last, step, 0)

    def look_all(places):
        def body(z):
            for t, j in places:
                look_up(z, t, j)

        over_slices(0, slices, body)

    def arrive(depth):
        for number in reversed(order):
            step = DIRS[number]
            if (step[0] != 0) != depth:
                continue

            @pl.when(there(tuple(-s for s in step)))
            def _():
                for copy in copies(number, step):
                    copy.wait_recv()

    def unpack(depth):
        for x in STEPS:
            first, last = (rows - halo, rows) if x > 0 else ((0, halo) if x < 0 else (0, rows))
            base = 0 if x > 0 else (high if x < 0 else low)
            if depth:
                jobs = [
                    (got_depth.at[slot, x + 1], wide_d.at[slot * (slices + 1)]) for slot in range(2)
                ]
                jobs = [(got.at[0], got.at[1], target) for got, target in jobs]
            else:
                jobs = [
                    (got.at[x + 1, 0, z], got.at[x + 1, 1, z], target.at[z + skip])
                    for got, target, skip in ((got_edges[0], wide_d, 1), (got_edges[1], wide_i, 0))
                    for z in range(slices)
                ]
            for from_left, from_right, target in jobs:
                left, right = from_left[...], from_right[...]
                for r in range(first // SUB, last // SUB):
                    a = (LANES - GROUP * r) % LANES
                    b = (LANES - GROUP - GROUP * r) % LANES
                    rr = pltpu.roll(right, a, 1) if a else right
                    ll = pltpu.roll(left, b, 1) if b else left
                    at = base + r * SUB - first
                    target[at:at + SUB, cols:wide] = jnp.where(lane < LANES // 2, rr, ll)

    look_all(own)
    arrive(False)
    unpack(False)
    look_all(rest)
    over_slices(1, slices - 1, slopes)
    arrive(True)
    unpack(True)
    slopes(0)
    if slices > 1:
        slopes(slices - 1)

    def partial(mask, first, last):
        view = flipped(d, mask)
        l0, l1, l2 = (light[view, k] for k in range(3))
        moves = []
        for z in range(slices):
            px = shear[view, 0, d * slices + z]
            py = shear[view, 1, d * slices + z]
            moves.append((
                MAXS - px, jnp.where(py < 0, py + LANES, py), lane < py, lane >= py + LANES,
            ))

        def rows_of(t, carry):
            acc = [[jnp.zeros((SUB, LANES), jnp.float32) for _ in range(tiles)] for _ in range(4)]
            for z in range(slices):
                start, turn, from_low, from_high = moves[z]
                at = pl.ds(start + t * SUB, SUB)
                bright = [
                    ambient + jnp.abs(
                        l0 * shaded[4, z, j, at, :] + l1 * shaded[5, z, j, at, :]
                        + l2 * shaded[6, z, j, at, :]
                    )
                    for j in range(tiles + 1)
                ]
                through = [1.0 - a for a in acc[0]]
                for ch in range(4):
                    turned = []
                    for j in range(tiles + 1):
                        v = shaded[ch, z, j, at, :]
                        turned.append(pltpu.roll(v * bright[j] if ch else v, turn, 1))
                    for j in range(tiles):
                        moved = jnp.where(
                            from_low, turned[j - 1],
                            jnp.where(from_high, turned[j + 1], turned[j]),
                        )
                        acc[ch][j] = acc[ch][j] + through[j] * moved
            r = pl.multiple_of(t * SUB, SUB)
            for ch in range(4):
                for j in range(tiles):
                    parts[mask, ch, pl.ds(r, SUB), j * LANES:(j + 1) * LANES] = acc[ch][j]
            return carry

        lax.fori_loop(first, last, rows_of, 0)

    sent = []
    halves = 4
    part = rows // halves

    def cut(h):
        return pl.ds(h * part, part)

    for h in range(halves):
        for mask in masks:
            partial(mask, h * part // SUB, (h + 1) * part // SUB)
            copy = pltpu.make_async_remote_copy(
                src_ref=parts.at[mask, :, cut(h), :], dst_ref=others.at[d, :, cut(h), :],
                send_sem=part_send.at[mask, h], recv_sem=part_recv.at[mask, h],
                device_id=(flipped(d, mask), me[1], me[2]), device_id_type=pl.DeviceIdType.MESH,
            )
            copy.start()
            sent.append(copy)
    partial(0, 0, rows // SUB)
    keep = pltpu.make_async_copy(parts.at[0], others.at[d], in_sem.at[0])
    keep.start()
    for number in order:
        step = DIRS[number]

        @pl.when(there(step))
        def _():
            for copy in copies(number, step):
                copy.wait_send()

    for copy in sent:
        copy.wait_recv()
    for copy in sent:
        copy.wait_send()
    keep.wait()


def local(sizes, density, table_index, opacity_table, color_table, light_direction, shear_offsets):
    slices, rows, cols = density.shape
    views = light_direction.shape[0]
    nd = sizes[0]
    assert views == nd and rows // SUB * GROUP == LANES
    wide = cols + LANES
    halo = -(-(MAXS + 1) // SUB) * SUB
    f32, i32 = jnp.float32, jnp.int32
    dma = pltpu.SemaphoreType.DMA
    turned = jnp.transpose(shear_offsets, (0, 2, 1))
    layers = pl.pallas_call(
        functools.partial(kernel, sizes),
        out_shape=pltpu.VMEM((nd, 4, rows, cols), f32),
        in_specs=[pl.BlockSpec(memory_space=pl.ANY)] * 6,
        out_specs=pl.BlockSpec(memory_space=pl.ANY),
        scratch_shapes=[
            pltpu.VMEM(opacity_table.shape, f32),
            pltpu.VMEM(color_table.shape, f32),
            pltpu.SMEM(light_direction.shape, f32),
            pltpu.SMEM(turned.shape, i32),
            dma((6,)),
            pltpu.VMEM((slices + 2, rows + 2 * halo, wide), f32),
            pltpu.VMEM((slices, rows + 2 * halo, wide), i32),
            [pltpu.VMEM((2, slices, SUB, LANES), f32), pltpu.VMEM((2, slices, SUB, LANES), i32)],
            [pltpu.VMEM((3, 2, slices, SUB, LANES), f32), pltpu.VMEM((3, 2, slices, SUB, LANES), i32)],
            pltpu.VMEM((2, 3, 2, SUB, LANES), f32),
            pltpu.VMEM((7, slices, wide // LANES, rows + 2 * MAXS, LANES), f32),
            pltpu.VMEM((nd, 4, rows, cols), f32),
            dma((len(DIRS),)), dma((len(DIRS),)), dma((len(DIRS),)), dma((len(DIRS),)),
            dma((nd, 4)), dma((nd, 4)),
        ],
        compiler_params=pltpu.CompilerParams(
            collective_id=0, has_side_effects=True
        ),
    )(density, table_index, opacity_table, color_table, light_direction, turned)
    image = layers[0:1]
    for k in range(1, nd):
        image = image + (1.0 - image[:, 0:1]) * layers[k:k + 1]
    return image


def solution(mesh):
    sizes = tuple(mesh.shape[name] for name in ("depth", "gx", "gy"))
    return jax.shard_map(
        functools.partial(local, sizes),
        mesh=mesh,
        in_specs=(P("depth", "gx", "gy"), P("depth", "gx", "gy"), P(), P(), P(), P()),
        out_specs=P("depth", None, "gx", "gy"),
        check_vma=False,
    )
```

```python
import functools

import jax
import jax.numpy as jnp
from jax import lax
from jax.experimental import pallas as pl
from jax.experimental.pallas import tpu as pltpu
from jax.sharding import PartitionSpec as P

MAXS = 16
LANES = 128
SUB = 8
GROUP = 32

ambient = 0.3
diffuse = 0.7

STEPS = (-1, 0, 1)
DIRS = [(z, x, y) for z in STEPS for x in STEPS for y in STEPS if (z, x, y) != (0, 0, 0)]


def flipped(value, mask):
    bit = 1
    while bit <= mask:
        if mask & bit:
            value = value + bit - 2 * bit * ((value // bit) % 2)
        bit *= 2
    return value


def kernel(
    sizes, dens_in, index_in, opacity_in, color_in, light_in, shear_in, others,
    opacity, color, light, shear, in_sem, wide_d, wide_i, edges, got_edges, got_depth, shaded, parts,
    send_sem, recv_sem, send2, recv2, part_send, part_recv,
):
    nd, nx, ny = sizes
    slices, rows, cols = dens_in.shape
    tiles = cols // LANES
    wide = cols + LANES
    halo = -(-(MAXS + 1) // SUB) * SUB
    low, high = halo, halo + rows
    me = (lax.axis_index("depth"), lax.axis_index("gx"), lax.axis_index("gy"))
    d = me[0]

    def there(step):
        ok = None
        for pos, s, n in zip(me, step, sizes):
            if s:
                one = (pos + s < n) if s > 0 else (pos + s >= 0)
                ok = one if ok is None else jnp.logical_and(ok, one)
        return ok

    def dev(step):
        return tuple(pos + s for pos, s in zip(me, step))

    masks = list(range(nd - 1, 0, -1))
    direct = [step for step in DIRS if step[0] == 0 or step[1] == 0 or step[2] != 0]
    barrier = pltpu.get_barrier_semaphore()
    count = jnp.int32(0)
    for step in direct:
        ok = there(step)

        @pl.when(ok)
        def _():
            pl.semaphore_signal(barrier, inc=1, device_id=dev(step), device_id_type=pl.DeviceIdType.MESH)

        count = count + jnp.where(ok, 1, 0)
    for mask in masks:
        gap = flipped(d, mask) - d
        far = jnp.logical_or(gap > 1, gap < -1)

        @pl.when(far)
        def _():
            pl.semaphore_signal(
                barrier, inc=1, device_id=(flipped(d, mask), me[1], me[2]),
                device_id_type=pl.DeviceIdType.MESH,
            )

        count = count + jnp.where(far, 1, 0)

    dens = wide_d.at[pl.ds(1, slices), pl.ds(low, rows), pl.ds(0, cols)]
    index = wide_i.at[:, pl.ds(low, rows), pl.ds(0, cols)]
    loads = [
        pltpu.make_async_copy(src, dst, in_sem.at[k])
        for k, (src, dst) in enumerate((
            (dens_in, dens), (index_in, index), (opacity_in, opacity), (color_in, color),
            (light_in, light), (shear_in, shear),
        ))
    ]
    for load in loads:
        load.start()
    loads[0].wait()
    loads[1].wait()
    lane = lax.broadcasted_iota(jnp.int32, (SUB, LANES), 1)
    group = lane // GROUP
    for side in range(2):
        tile = tiles - 1 if side == 0 else 0
        for number, (ref, buf) in enumerate(((wide_d, 0), (wide_i, 1))):
            for z in range(slices):
                packed = None
                for r in range(rows // SUB):
                    v = ref[z + 1 - buf, low + r * SUB:low + (r + 1) * SUB, tile * LANES:(tile + 1) * LANES]
                    shift = (GROUP * r + (GROUP if side == 0 else 0)) % LANES
                    v = pltpu.roll(v, shift, 1) if shift else v
                    packed = v if packed is None else jnp.where(group == r, v, packed)
                edges[buf][side, z] = packed

    def src_rows(x, reach):
        return pl.ds(high - reach, reach) if x > 0 else (pl.ds(low, reach) if x < 0 else pl.ds(low, rows))

    def dst_rows(x, reach):
        return pl.ds(low - reach, reach) if x > 0 else (pl.ds(high, reach) if x < 0 else pl.ds(low, rows))

    def copies(number, step, only_dst=False):
        z, x, y = step
        relay = step not in direct
        side = 0 if y > 0 else 1
        edge = slices - 1 if z > 0 else 0
        slot = 0 if z > 0 else 1
        put = 0 if z > 0 else slices + 1
        if z == 0 and y == 0:
            pairs = [
                (wide_d.at[pl.ds(1, slices), src_rows(x, halo), pl.ds(0, cols)],
                 wide_d.at[pl.ds(1, slices), dst_rows(x, halo), pl.ds(0, cols)]),
                (wide_i.at[:, src_rows(x, MAXS), pl.ds(0, cols)], wide_i.at[:, dst_rows(x, MAXS), pl.ds(0, cols)]),
            ]
        elif z == 0:
            pairs = [
                (got.at[1, side] if relay else own_edges.at[side], got.at[x + 1, side])
                for own_edges, got in zip(edges, got_edges)
            ]
        elif y == 0:
            pairs = [(
                wide_d.at[put if relay else edge + 1, src_rows(x, MAXS), pl.ds(0, cols)],
                wide_d.at[put, dst_rows(x, MAXS), pl.ds(0, cols)],
            )]
        else:
            pairs = [(
                got_depth.at[slot, 1, side] if relay else edges[0].at[side, edge], got_depth.at[slot, x + 1, side],
            )]
        if only_dst:
            return [dst for _src, dst in pairs]
        made = []
        for (src, dst), (ss, rs) in zip(pairs, ((send_sem, recv_sem), (send2, recv2))):
            made.append(pltpu.make_async_remote_copy(
                src_ref=src, dst_ref=dst, send_sem=ss.at[number], recv_sem=rs.at[number],
                device_id=dev((0, x, 0) if relay else step), device_id_type=pl.DeviceIdType.MESH,
            ))
        return made

    def sends(step):
        if step in direct:
            return there(step)
        z, x, y = step
        return jnp.logical_and(there((0, x, 0)), there((-z, 0, -y)))

    def launch(steps):
        for step in steps:
            @pl.when(sends(step))
            def _():
                for copy in copies(DIRS.index(step), step):
                    copy.start()

    def arrive(steps):
        for step in steps:
            @pl.when(there(tuple(-s for s in step)))
            def _():
                for copy in copies(DIRS.index(step), step):
                    copy.wait_recv()

    def relays(z, y):
        return [(z, x, y) for x in (-1, 1)]

    def relay(steps):
        launch([step for step in steps if step not in direct])

    pl.semaphore_wait(barrier, count)
    launch(sorted(direct, key=lambda step: -sum(abs(s) for s in step)))

    for number, step in enumerate(DIRS):
        back = tuple(-s for s in step)

        @pl.when(jnp.logical_not(there(back)))
        def _():
            for dst in copies(number, step, only_dst=True):
                dst[...] = jnp.zeros(dst.shape, dst.dtype)

    for load in loads[2:]:
        load.wait()

    entries = opacity.shape[0] // LANES
    tables = []
    for name in range(4):
        halves = []
        for e in range(entries):
            if name == 0:
                row = opacity[e * LANES:(e + 1) * LANES].reshape(1, LANES)
            else:
                row = color[name - 1:name, e * LANES:(e + 1) * LANES]
            halves.append(jnp.broadcast_to(row, (SUB, LANES)))
        tables.append(halves)

    def look(name, low_bits, part):
        value = None
        for e in range(entries):
            g = jnp.take_along_axis(tables[name][e], low_bits, axis=1, mode="promise_in_bounds")
            value = g if value is None else jnp.where(part >= e, g, value)
        return value

    offset = halo - MAXS

    def look_up(z, t, j):
        at = offset + t * SUB
        r0 = t * SUB
        cut = slice(j * LANES, (j + 1) * LANES)
        i = wide_i[z, at:at + SUB, cut]
        low_bits = jnp.bitwise_and(i, LANES - 1)
        part = jnp.right_shift(i, 7)
        alpha = 1.0 - jnp.exp(-look(0, low_bits, part) * wide_d[z + 1, at:at + SUB, cut])
        shaded[0, z, j, r0:r0 + SUB, :] = alpha
        for ch in range(3):
            shaded[1 + ch, z, j, r0:r0 + SUB, :] = alpha * look(1 + ch, low_bits, part)

    def slopes(z):
        for t in range(wide_tiles):
            at = offset + t * SUB
            r0 = t * SUB
            c = wide_d[z + 1, at:at + SUB, :]
            sd = wide_d[z + 2, at:at + SUB, :] - wide_d[z, at:at + SUB, :]
            sx = wide_d[z + 1, at + 1:at + 1 + SUB, :] - wide_d[z + 1, at - 1:at - 1 + SUB, :]
            sy = pltpu.roll(c, wide - 1, 1) - pltpu.roll(c, 1, 1)
            inv = lax.rsqrt(0.25 * (sd * sd + sx * sx + sy * sy) + 1.0) * (0.5 * diffuse)
            for j in range(wide // LANES):
                for k, slope in enumerate((sd, sx, sy)):
                    shaded[4 + k, z, j, r0:r0 + SUB, :] = (slope * inv)[:, j * LANES:(j + 1) * LANES]

    wide_tiles = (rows + 2 * MAXS) // SUB
    own = [
        (t, j) for t in range(MAXS // SUB, (MAXS + rows) // SUB) for j in range(tiles)
    ]
    beside = [(t, j) for t in range(wide_tiles) for j in range(tiles) if (t, j) not in own]
    edge_own = [(t, tiles) for t in range(MAXS // SUB, (MAXS + rows) // SUB)]
    edge_rest = [(t, tiles) for t in range(wide_tiles) if (t, tiles) not in edge_own]

    def over_slices(first, last, body):
        def step(z, carry):
            body(z)
            return carry

        lax.fori_loop(first, last, step, 0)

    def look_all(places):
        def body(z):
            for t, j in places:
                look_up(z, t, j)

        over_slices(0, slices, body)

    def unpack(depth, steps):
        for x in steps:
            first, last = (rows - halo, rows) if x > 0 else ((0, halo) if x < 0 else (0, rows))
            base = 0 if x > 0 else (high if x < 0 else low)
            if depth:
                jobs = [
                    (got_depth.at[slot, x + 1], wide_d.at[slot * (slices + 1)]) for slot in range(2)
                ]
                jobs = [(got.at[0], got.at[1], target) for got, target in jobs]
            else:
                jobs = [
                    (got.at[x + 1, 0, z], got.at[x + 1, 1, z], target.at[z + skip])
                    for got, target, skip in ((got_edges[0], wide_d, 1), (got_edges[1], wide_i, 0))
                    for z in range(slices)
                ]
            for from_left, from_right, target in jobs:
                left, right = from_left[...], from_right[...]
                for r in range(first // SUB, last // SUB):
                    a = (LANES - GROUP * r) % LANES
                    b = (LANES - GROUP - GROUP * r) % LANES
                    rr = pltpu.roll(right, a, 1) if a else right
                    ll = pltpu.roll(left, b, 1) if b else left
                    at = base + r * SUB - first
                    target[at:at + SUB, cols:wide] = jnp.where(lane < LANES // 2, rr, ll)

    look_all(own)
    arrive([(0, x, 0) for x in (-1, 1)])
    look_all(beside)
    arrive([(z, 0, 0) for z in (-1, 1)])
    relay(relays(-1, 0) + relays(1, 0))
    for y in (-1, 1):
        arrive([(0, 0, y)])
        relay(relays(0, y))
    unpack(False, (0,))
    look_all(edge_own)
    for z in (-1, 1):
        for y in (-1, 1):
            arrive([(z, 0, y)])
            relay(relays(z, y))
    arrive(relays(0, -1) + relays(0, 1))
    unpack(False, (-1, 1))
    look_all(edge_rest)
    over_slices(1, slices - 1, slopes)
    arrive([step for z in (-1, 1) for y in STEPS for step in relays(z, y)])
    unpack(True, STEPS)
    slopes(0)
    if slices > 1:
        slopes(slices - 1)

    def partial(mask, first, last):
        view = flipped(d, mask)
        l0, l1, l2 = (light[view, k] for k in range(3))
        moves = []
        for z in range(slices):
            px = shear[view, 0, d * slices + z]
            py = shear[view, 1, d * slices + z]
            moves.append((
                MAXS - px, jnp.where(py < 0, py + LANES, py), lane < py, lane >= py + LANES,
            ))

        def rows_of(t, carry):
            acc = [[jnp.zeros((SUB, LANES), jnp.float32) for _ in range(tiles)] for _ in range(4)]
            for z in range(slices):
                start, turn, from_low, from_high = moves[z]
                at = pl.ds(start + t * SUB, SUB)
                bright = [
                    ambient + jnp.abs(
                        l0 * shaded[4, z, j, at, :] + l1 * shaded[5, z, j, at, :]
                        + l2 * shaded[6, z, j, at, :]
                    )
                    for j in range(tiles + 1)
                ]
                through = [1.0 - a for a in acc[0]]
                for ch in range(4):
                    turned = []
                    for j in range(tiles + 1):
                        v = shaded[ch, z, j, at, :]
                        turned.append(pltpu.roll(v * bright[j] if ch else v, turn, 1))
                    for j in range(tiles):
                        moved = jnp.where(
                            from_low, turned[j - 1],
                            jnp.where(from_high, turned[j + 1], turned[j]),
                        )
                        acc[ch][j] = acc[ch][j] + through[j] * moved
            r = pl.multiple_of(t * SUB, SUB)
            for ch in range(4):
                for j in range(tiles):
                    parts[mask, ch, pl.ds(r, SUB), j * LANES:(j + 1) * LANES] = acc[ch][j]
            return carry

        lax.fori_loop(first, last, rows_of, 0)

    sent = []
    halves = 4
    part = rows // halves

    def cut(h):
        return pl.ds(h * part, part)

    for h in range(halves):
        for mask in masks:
            partial(mask, h * part // SUB, (h + 1) * part // SUB)
            copy = pltpu.make_async_remote_copy(
                src_ref=parts.at[mask, :, cut(h), :], dst_ref=others.at[d, :, cut(h), :],
                send_sem=part_send.at[mask, h], recv_sem=part_recv.at[mask, h],
                device_id=(flipped(d, mask), me[1], me[2]), device_id_type=pl.DeviceIdType.MESH,
            )
            copy.start()
            sent.append(copy)
    partial(0, 0, rows // SUB)
    keep = pltpu.make_async_copy(parts.at[0], others.at[d], in_sem.at[0])
    keep.start()
    for number, step in enumerate(DIRS):
        @pl.when(sends(step))
        def _():
            for copy in copies(number, step):
                copy.wait_send()

    for copy in sent:
        copy.wait_recv()
    for copy in sent:
        copy.wait_send()
    keep.wait()


def local(sizes, density, table_index, opacity_table, color_table, light_direction, shear_offsets):
    slices, rows, cols = density.shape
    views = light_direction.shape[0]
    nd = sizes[0]
    assert views == nd and rows // SUB * GROUP == LANES
    wide = cols + LANES
    halo = -(-(MAXS + 1) // SUB) * SUB
    f32, i32 = jnp.float32, jnp.int32
    dma = pltpu.SemaphoreType.DMA
    turned = jnp.transpose(shear_offsets, (0, 2, 1))
    layers = pl.pallas_call(
        functools.partial(kernel, sizes),
        out_shape=pltpu.VMEM((nd, 4, rows, cols), f32),
        in_specs=[pl.BlockSpec(memory_space=pl.ANY)] * 6,
        out_specs=pl.BlockSpec(memory_space=pl.ANY),
        scratch_shapes=[
            pltpu.VMEM(opacity_table.shape, f32),
            pltpu.VMEM(color_table.shape, f32),
            pltpu.SMEM(light_direction.shape, f32),
            pltpu.SMEM(turned.shape, i32),
            dma((6,)),
            pltpu.VMEM((slices + 2, rows + 2 * halo, wide), f32),
            pltpu.VMEM((slices, rows + 2 * halo, wide), i32),
            [pltpu.VMEM((2, slices, SUB, LANES), f32), pltpu.VMEM((2, slices, SUB, LANES), i32)],
            [pltpu.VMEM((3, 2, slices, SUB, LANES), f32), pltpu.VMEM((3, 2, slices, SUB, LANES), i32)],
            pltpu.VMEM((2, 3, 2, SUB, LANES), f32),
            pltpu.VMEM((7, slices, wide // LANES, rows + 2 * MAXS, LANES), f32),
            pltpu.VMEM((nd, 4, rows, cols), f32),
            dma((len(DIRS),)), dma((len(DIRS),)), dma((len(DIRS),)), dma((len(DIRS),)),
            dma((nd, 4)), dma((nd, 4)),
        ],
        compiler_params=pltpu.CompilerParams(
            collective_id=0, has_side_effects=True
        ),
    )(density, table_index, opacity_table, color_table, light_direction, turned)
    image = layers[0:1]
    for k in range(1, nd):
        image = image + (1.0 - image[:, 0:1]) * layers[k:k + 1]
    return image


def solution(mesh):
    sizes = tuple(mesh.shape[name] for name in ("depth", "gx", "gy"))
    return jax.shard_map(
        functools.partial(local, sizes),
        mesh=mesh,
        in_specs=(P("depth", "gx", "gy"), P("depth", "gx", "gy"), P(), P(), P(), P()),
        out_specs=P("depth", None, "gx", "gy"),
        check_vma=False,
    )
```

```python
import functools

import jax
import jax.numpy as jnp
from jax import lax
from jax.experimental import pallas as pl
from jax.experimental.pallas import tpu as pltpu
from jax.sharding import PartitionSpec as P

MAXS = 16
LANES = 128
SUB = 8
GROUP = 32

ambient = 0.3
diffuse = 0.7

STEPS = (-1, 0, 1)
DIRS = [(z, x, y) for z in STEPS for x in STEPS for y in STEPS if (z, x, y) != (0, 0, 0)]


def flipped(value, mask):
    bit = 1
    while bit <= mask:
        if mask & bit:
            value = value + bit - 2 * bit * ((value // bit) % 2)
        bit *= 2
    return value


def kernel(
    sizes, dens_in, index_in, opacity_in, color_in, light_in, shear_in, others,
    opacity, color, light, shear, in_sem, wide_d, wide_i, edges, ends, got_edges, got_depth, shaded, parts,
    send_sem, recv_sem, send2, recv2, part_send, part_recv,
):
    nd, nx, ny = sizes
    slices, rows, cols = dens_in.shape
    tiles = cols // LANES
    wide = cols + LANES
    halo = -(-(MAXS + 1) // SUB) * SUB
    low, high = halo, halo + rows
    me = (lax.axis_index("depth"), lax.axis_index("gx"), lax.axis_index("gy"))
    d = me[0]

    def there(step):
        ok = None
        for pos, s, n in zip(me, step, sizes):
            if s:
                one = (pos + s < n) if s > 0 else (pos + s >= 0)
                ok = one if ok is None else jnp.logical_and(ok, one)
        return ok

    def dev(step):
        return tuple(pos + s for pos, s in zip(me, step))

    masks = list(range(nd - 1, 0, -1))
    direct = [step for step in DIRS if step[0] == 0 or step[1] == 0 or step[2] != 0]
    barrier = pltpu.get_barrier_semaphore()
    count = jnp.int32(0)
    for step in direct:
        ok = there(step)

        @pl.when(ok)
        def _():
            pl.semaphore_signal(barrier, inc=1, device_id=dev(step), device_id_type=pl.DeviceIdType.MESH)

        count = count + jnp.where(ok, 1, 0)
    for mask in masks:
        gap = flipped(d, mask) - d
        far = jnp.logical_or(gap > 1, gap < -1)

        @pl.when(far)
        def _():
            pl.semaphore_signal(
                barrier, inc=1, device_id=(flipped(d, mask), me[1], me[2]),
                device_id_type=pl.DeviceIdType.MESH,
            )

        count = count + jnp.where(far, 1, 0)

    dens = wide_d.at[pl.ds(1, slices), pl.ds(low, rows), pl.ds(0, cols)]
    index = wide_i.at[:, pl.ds(low, rows), pl.ds(0, cols)]
    loads = [
        pltpu.make_async_copy(src, dst, in_sem.at[k])
        for k, (src, dst) in enumerate((
            (dens_in, dens), (index_in, index), (opacity_in, opacity), (color_in, color),
            (light_in, light), (shear_in, shear),
        ))
    ]
    for load in loads:
        load.start()
    loads[0].wait()
    loads[1].wait()
    lane = lax.broadcasted_iota(jnp.int32, (SUB, LANES), 1)
    group = lane // GROUP
    for side in range(2):
        tile = tiles - 1 if side == 0 else 0
        for ref, buf in ((wide_d, 0), (wide_i, 1)):
            last = [None, None]
            for r in range(rows // SUB):
                packed = None
                for z in range(slices):
                    v = ref[z + 1 - buf, low + r * SUB:low + (r + 1) * SUB, tile * LANES:(tile + 1) * LANES]
                    for place, into in ((z, None),) + ((((r, 0),) if z == 0 else ()) + (((r, 1),) if z == slices - 1 else ()) if buf == 0 else ()):
                        shift = (GROUP * place + (GROUP if side == 0 else 0)) % LANES
                        w = pltpu.roll(v, shift, 1) if shift else v
                        if into is None:
                            packed = w if packed is None else jnp.where(group == place, w, packed)
                        else:
                            last[into] = w if last[into] is None else jnp.where(group == place, w, last[into])
                edges[buf][side, r] = packed
            if buf == 0:
                for into in range(2):
                    ends[side, into] = last[into]

    def tiles_of(x, reach):
        n = reach // SUB
        return pl.ds(rows // SUB - n, n) if x > 0 else (pl.ds(0, n) if x < 0 else pl.ds(0, rows // SUB))

    def src_rows(x, reach):
        return pl.ds(high - reach, reach) if x > 0 else (pl.ds(low, reach) if x < 0 else pl.ds(low, rows))

    def dst_rows(x, reach):
        return pl.ds(low - reach, reach) if x > 0 else (pl.ds(high, reach) if x < 0 else pl.ds(low, rows))

    def copies(number, step, only_dst=False):
        z, x, y = step
        relay = step not in direct
        side = 0 if y > 0 else 1
        edge = slices - 1 if z > 0 else 0
        slot = 0 if z > 0 else 1
        put = 0 if z > 0 else slices + 1
        if z == 0 and y == 0:
            pairs = [
                (wide_d.at[pl.ds(1, slices), src_rows(x, halo), pl.ds(0, cols)],
                 wide_d.at[pl.ds(1, slices), dst_rows(x, halo), pl.ds(0, cols)]),
                (wide_i.at[:, src_rows(x, MAXS), pl.ds(0, cols)], wide_i.at[:, dst_rows(x, MAXS), pl.ds(0, cols)]),
            ]
        elif z == 0:
            pairs = [
                (own_edges.at[side, tiles_of(x, reach)], got.at[x + 1, side, tiles_of(x, reach)])
                for own_edges, got, reach in zip(edges, got_edges, (halo, MAXS))
            ]
        elif y == 0:
            pairs = [(
                wide_d.at[put if relay else edge + 1, src_rows(x, MAXS), pl.ds(0, cols)],
                wide_d.at[put, dst_rows(x, MAXS), pl.ds(0, cols)],
            )]
        else:
            pairs = [(
                got_depth.at[slot, 1, side] if relay else ends.at[side, 1 if z > 0 else 0], got_depth.at[slot, x + 1, side],
            )]
        if only_dst:
            return [dst for _src, dst in pairs]
        made = []
        for (src, dst), (ss, rs) in zip(pairs, ((send_sem, recv_sem), (send2, recv2))):
            made.append(pltpu.make_async_remote_copy(
                src_ref=src, dst_ref=dst, send_sem=ss.at[number], recv_sem=rs.at[number],
                device_id=dev((0, x, 0) if relay else step), device_id_type=pl.DeviceIdType.MESH,
            ))
        return made

    def sends(step):
        if step in direct:
            return there(step)
        z, x, y = step
        return jnp.logical_and(there((0, x, 0)), there((-z, 0, -y)))

    def launch(steps):
        for step in steps:
            @pl.when(sends(step))
            def _():
                for copy in copies(DIRS.index(step), step):
                    copy.start()

    def arrive(steps):
        for step in steps:
            @pl.when(there(tuple(-s for s in step)))
            def _():
                for copy in copies(DIRS.index(step), step):
                    copy.wait_recv()

    def relays(z, y):
        return [(z, x, y) for x in (-1, 1)]

    def relay(steps):
        launch([step for step in steps if step not in direct])

    pl.semaphore_wait(barrier, count)
    launch(sorted(direct, key=lambda step: -sum(abs(s) for s in step)))

    for number, step in enumerate(DIRS):
        back = tuple(-s for s in step)

        @pl.when(jnp.logical_not(there(back)))
        def _():
            for dst in copies(number, step, only_dst=True):
                dst[...] = jnp.zeros(dst.shape, dst.dtype)

    for load in loads[2:]:
        load.wait()

    entries = opacity.shape[0] // LANES
    tables = []
    for name in range(4):
        halves = []
        for e in range(entries):
            if name == 0:
                row = opacity[e * LANES:(e + 1) * LANES].reshape(1, LANES)
            else:
                row = color[name - 1:name, e * LANES:(e + 1) * LANES]
            halves.append(jnp.broadcast_to(row, (SUB, LANES)))
        tables.append(halves)

    def look(name, low_bits, part):
        value = None
        for e in range(entries):
            g = jnp.take_along_axis(tables[name][e], low_bits, axis=1, mode="promise_in_bounds")
            value = g if value is None else jnp.where(part >= e, g, value)
        return value

    offset = halo - MAXS

    def look_up(z, t, j):
        at = offset + t * SUB
        r0 = t * SUB
        cut = slice(j * LANES, (j + 1) * LANES)
        i = wide_i[z, at:at + SUB, cut]
        low_bits = jnp.bitwise_and(i, LANES - 1)
        part = jnp.right_shift(i, 7)
        alpha = 1.0 - jnp.exp(-look(0, low_bits, part) * wide_d[z + 1, at:at + SUB, cut])
        shaded[0, z, j, r0:r0 + SUB, :] = alpha
        for ch in range(3):
            shaded[1 + ch, z, j, r0:r0 + SUB, :] = alpha * look(1 + ch, low_bits, part)

    def slopes(z):
        for t in range(wide_tiles):
            at = offset + t * SUB
            r0 = t * SUB
            c = wide_d[z + 1, at:at + SUB, :]
            sd = wide_d[z + 2, at:at + SUB, :] - wide_d[z, at:at + SUB, :]
            sx = wide_d[z + 1, at + 1:at + 1 + SUB, :] - wide_d[z + 1, at - 1:at - 1 + SUB, :]
            sy = pltpu.roll(c, wide - 1, 1) - pltpu.roll(c, 1, 1)
            inv = lax.rsqrt(0.25 * (sd * sd + sx * sx + sy * sy) + 1.0) * (0.5 * diffuse)
            for j in range(wide // LANES):
                for k, slope in enumerate((sd, sx, sy)):
                    shaded[4 + k, z, j, r0:r0 + SUB, :] = (slope * inv)[:, j * LANES:(j + 1) * LANES]

    wide_tiles = (rows + 2 * MAXS) // SUB
    own = [
        (t, j) for t in range(MAXS // SUB, (MAXS + rows) // SUB) for j in range(tiles)
    ]
    beside = [(t, j) for t in range(wide_tiles) for j in range(tiles) if (t, j) not in own]
    edge_own = [(t, tiles) for t in range(MAXS // SUB, (MAXS + rows) // SUB)]
    edge_rest = [(t, tiles) for t in range(wide_tiles) if (t, tiles) not in edge_own]

    def over_slices(first, last, body):
        def step(z, carry):
            body(z)
            return carry

        lax.fori_loop(first, last, step, 0)

    def look_all(places):
        def body(z):
            for t, j in places:
                look_up(z, t, j)

        over_slices(0, slices, body)

    def unpack(depth, steps):
        for x in steps:
            first, last = (rows - halo, rows) if x > 0 else ((0, halo) if x < 0 else (0, rows))
            base = 0 if x > 0 else (high if x < 0 else low)
            jobs = []
            for r in range(first // SUB, last // SUB):
                at = base + r * SUB - first
                if depth:
                    jobs += [
                        (got_depth.at[slot, x + 1, 0], got_depth.at[slot, x + 1, 1], r, wide_d.at[slot * (slices + 1)], at)
                        for slot in range(2)
                    ]
                    continue
                for got, target, skip, reach in ((got_edges[0], wide_d, 1, halo), (got_edges[1], wide_i, 0, MAXS)):
                    if (x > 0 and r < (rows - reach) // SUB) or (x < 0 and r >= reach // SUB):
                        continue
                    jobs += [
                        (got.at[x + 1, 0, r], got.at[x + 1, 1, r], z, target.at[z + skip], at) for z in range(slices)
                    ]
            for from_left, from_right, place, target, at in jobs:
                left, right = from_left[...], from_right[...]
                a = (LANES - GROUP * place) % LANES
                b = (LANES - GROUP - GROUP * place) % LANES
                rr = pltpu.roll(right, a, 1) if a else right
                ll = pltpu.roll(left, b, 1) if b else left
                target[at:at + SUB, cols:wide] = jnp.where(lane < LANES // 2, rr, ll)

    look_all(own)
    arrive([(0, x, 0) for x in (-1, 1)])
    look_all(beside)
    arrive([(z, 0, 0) for z in (-1, 1)])
    relay(relays(-1, 0) + relays(1, 0))
    for y in (-1, 1):
        arrive([(0, 0, y)])
        relay(relays(0, y))
    unpack(False, (0,))
    look_all(edge_own)
    for z in (-1, 1):
        for y in (-1, 1):
            arrive([(z, 0, y)])
            relay(relays(z, y))
    arrive(relays(0, -1) + relays(0, 1))
    unpack(False, (-1, 1))
    look_all(edge_rest)
    over_slices(1, slices - 1, slopes)
    arrive([step for z in (-1, 1) for y in STEPS for step in relays(z, y)])
    unpack(True, STEPS)
    slopes(0)
    if slices > 1:
        slopes(slices - 1)

    def partial(mask, first, last):
        view = flipped(d, mask)
        l0, l1, l2 = (light[view, k] for k in range(3))
        moves = []
        for z in range(slices):
            px = shear[view, 0, d * slices + z]
            py = shear[view, 1, d * slices + z]
            moves.append((
                MAXS - px, jnp.where(py < 0, py + LANES, py), lane < py, lane >= py + LANES,
            ))

        def rows_of(t, carry):
            acc = [[jnp.zeros((SUB, LANES), jnp.float32) for _ in range(tiles)] for _ in range(4)]
            for z in range(slices):
                start, turn, from_low, from_high = moves[z]
                at = pl.ds(start + t * SUB, SUB)
                bright = [
                    ambient + jnp.abs(
                        l0 * shaded[4, z, j, at, :] + l1 * shaded[5, z, j, at, :]
                        + l2 * shaded[6, z, j, at, :]
                    )
                    for j in range(tiles + 1)
                ]
                through = [1.0 - a for a in acc[0]]
                for ch in range(4):
                    turned = []
                    for j in range(tiles + 1):
                        v = shaded[ch, z, j, at, :]
                        turned.append(pltpu.roll(v * bright[j] if ch else v, turn, 1))
                    for j in range(tiles):
                        moved = jnp.where(
                            from_low, turned[j - 1],
                            jnp.where(from_high, turned[j + 1], turned[j]),
                        )
                        acc[ch][j] = acc[ch][j] + through[j] * moved
            r = pl.multiple_of(t * SUB, SUB)
            for ch in range(4):
                for j in range(tiles):
                    parts[mask, ch, pl.ds(r, SUB), j * LANES:(j + 1) * LANES] = acc[ch][j]
            return carry

        lax.fori_loop(first, last, rows_of, 0)

    sent = []
    halves = 4
    part = rows // halves

    def cut(h):
        return pl.ds(h * part, part)

    for h in range(halves):
        for mask in masks:
            partial(mask, h * part // SUB, (h + 1) * part // SUB)
            copy = pltpu.make_async_remote_copy(
                src_ref=parts.at[mask, :, cut(h), :], dst_ref=others.at[d, :, cut(h), :],
                send_sem=part_send.at[mask, h], recv_sem=part_recv.at[mask, h],
                device_id=(flipped(d, mask), me[1], me[2]), device_id_type=pl.DeviceIdType.MESH,
            )
            copy.start()
            sent.append(copy)
    partial(0, 0, rows // SUB)
    keep = pltpu.make_async_copy(parts.at[0], others.at[d], in_sem.at[0])
    keep.start()
    for number, step in enumerate(DIRS):
        @pl.when(sends(step))
        def _():
            for copy in copies(number, step):
                copy.wait_send()

    for copy in sent:
        copy.wait_recv()
    for copy in sent:
        copy.wait_send()
    keep.wait()


def local(sizes, density, table_index, opacity_table, color_table, light_direction, shear_offsets):
    slices, rows, cols = density.shape
    views = light_direction.shape[0]
    nd = sizes[0]
    assert views == nd and rows // SUB * GROUP == LANES and slices * GROUP <= LANES
    wide = cols + LANES
    halo = -(-(MAXS + 1) // SUB) * SUB
    f32, i32 = jnp.float32, jnp.int32
    dma = pltpu.SemaphoreType.DMA
    turned = jnp.transpose(shear_offsets, (0, 2, 1))
    layers = pl.pallas_call(
        functools.partial(kernel, sizes),
        out_shape=pltpu.VMEM((nd, 4, rows, cols), f32),
        in_specs=[pl.BlockSpec(memory_space=pl.ANY)] * 6,
        out_specs=pl.BlockSpec(memory_space=pl.ANY),
        scratch_shapes=[
            pltpu.VMEM(opacity_table.shape, f32),
            pltpu.VMEM(color_table.shape, f32),
            pltpu.SMEM(light_direction.shape, f32),
            pltpu.SMEM(turned.shape, i32),
            dma((6,)),
            pltpu.VMEM((slices + 2, rows + 2 * halo, wide), f32),
            pltpu.VMEM((slices, rows + 2 * halo, wide), i32),
            [pltpu.VMEM((2, rows // SUB, SUB, LANES), f32), pltpu.VMEM((2, rows // SUB, SUB, LANES), i32)],
            pltpu.VMEM((2, 2, SUB, LANES), f32),
            [pltpu.VMEM((3, 2, rows // SUB, SUB, LANES), f32), pltpu.VMEM((3, 2, rows // SUB, SUB, LANES), i32)],
            pltpu.VMEM((2, 3, 2, SUB, LANES), f32),
            pltpu.VMEM((7, slices, wide // LANES, rows + 2 * MAXS, LANES), f32),
            pltpu.VMEM((nd, 4, rows, cols), f32),
            dma((len(DIRS),)), dma((len(DIRS),)), dma((len(DIRS),)), dma((len(DIRS),)),
            dma((nd, 4)), dma((nd, 4)),
        ],
        compiler_params=pltpu.CompilerParams(
            collective_id=0, has_side_effects=True
        ),
    )(density, table_index, opacity_table, color_table, light_direction, turned)
    image = layers[0:1]
    for k in range(1, nd):
        image = image + (1.0 - image[:, 0:1]) * layers[k:k + 1]
    return image


def solution(mesh):
    sizes = tuple(mesh.shape[name] for name in ("depth", "gx", "gy"))
    return jax.shard_map(
        functools.partial(local, sizes),
        mesh=mesh,
        in_specs=(P("depth", "gx", "gy"), P("depth", "gx", "gy"), P(), P(), P(), P()),
        out_specs=P("depth", None, "gx", "gy"),
        check_vma=False,
    )
```
